512 devices in a mesh: ctx: 32 (over x, y, core), mem: 16 (over z).
Axes of the slice: x: 4, y: 4, z: 16, core: 2. Of those that a mesh axis runs over, the one named last changes fastest.
Arguments:
- tokens: bfloat16 [131072, 1024], P(('ctx', 'mem')), may hold values from -36 to 36
- routes: int32 [131072, 2], P(('ctx', 'mem')), may hold values from 0 to 15, all different within a row; in each aligned block of 256 rows (0 to 255, 256 to 511, ...) at most 48 rows name the same one
- router: bfloat16 [1024, 16], replicated, may hold values from -0.1875 to 0.1875
- mem_weight: bfloat16 [16, 1024, 1536], P('mem'), may hold values from -0.1875 to 0.1875
- win_weight: bfloat16 [1024, 1536], P('mem'), may hold values from -3 to 3
Outputs:
- mixed: bfloat16 [131072, 512], P(('ctx', 'mem'))
The draws below stay inside these ranges and needn't reach their ends.
Inputs may be any that keep to these rules, and one draw needn't show every extreme that they name: `routes`: each token names 2 different memories; the 256 tokens of one device name any one memory at most 48 times.
All inputs are finite; a program needn't handle non-finite values.
Results may differ from the reference program's by a relative error of at most 0.009.
Values may be sent and summed in bfloat16 or wider, within the bound.
A program may use at most 64 MiB of HBM per device.

```python
import math
import jax
import jax.numpy as jnp
import numpy as np
from jax import lax

D = 1024
HEADS = 4
HDIM = 128
TOP = 2
WINDOW = 512
TOK_DEV = 256
MEMS = 16
CAP = 48
TOKENS = 131072
N_CTX = 32
N_MEM = 16


def draw_tokens(key, part):
    first_key = jax.random.fold_in(key, 11)
    base = jnp.clip(jax.random.normal(first_key, (TOKENS, D), jnp.float32), -6.0, 6.0)
    values = base
    return values.astype(jnp.bfloat16)


def draw_win_weight(key, part):
    width = HEADS * HDIM
    spread = D ** (-0.5)
    raw = jnp.clip(jax.random.normal(jax.random.fold_in(key, 21), (D, 3, width), jnp.float32), -6.0, 6.0) * spread
    values = raw.reshape(D, 3 * width)
    return values.astype(jnp.bfloat16)


def block_levels(stream_key, shape, cuts, least, top_value):
    factor_of = 1.0
    for dim, parts in cuts:
        draws = jax.random.uniform(jax.random.fold_in(jax.random.fold_in(stream_key, 6), dim), (parts,), jnp.float32, least / len(cuts), top_value / len(cuts))
        factor_of = factor_of * jnp.repeat(jnp.exp(draws), shape[dim] // parts).reshape((-1,) + (1,) * (len(shape) - 1 - dim))
    return factor_of


def assign_block(key, own, number, rows, number_of, top, bound, lean):
    order = jax.random.permutation(key, number_of)
    crowded, common = load_shares(number_of, rows * top, bound, lean, True), load_shares(number_of, rows * top, bound, lean, False)
    places = jnp.arange(number_of)

    def named(lengths, offset_by):
        used = int((lengths > 0).sum())
        fixed = max(1, used // 4)
        passed = fixed + (places - fixed + offset_by * (used - fixed)) % max(1, number_of - fixed)
        return jnp.zeros((number_of,), jnp.int32).at[order[jnp.where(places < fixed, places, passed)]].set(jnp.asarray(lengths, jnp.int32))

    lengths = jnp.where(number % 4 == 0, named(crowded, number // 4), named(common, number - number // 4 - 1))
    mixed = jax.random.permutation(jax.random.fold_in(own, 3), number_of)
    source_of, taker = mixed[0:number_of // 2 * 2:2], mixed[1:number_of // 2 * 2:2]
    margin = jnp.minimum(lengths[source_of] - 1, bound - lengths[taker]) // 2
    margin = jnp.where((source_of == order[0]) | (taker == order[0]) | (lengths[taker] == 0), 0, jnp.maximum(margin, 0))
    passed = jax.random.randint(jax.random.fold_in(own, 4), (number_of // 2,), 0, 1 << 20) % (margin + 1)
    lengths = lengths.at[source_of].add(-passed).at[taker].add(passed)
    members = jnp.searchsorted(jnp.cumsum(lengths), jnp.arange(rows * top), side="right").astype(jnp.int32)
    table = members.reshape(top, rows).T
    table = table[jax.random.permutation(jax.random.fold_in(own, 1), rows)]
    offset_by = jax.random.randint(jax.random.fold_in(own, 2), (rows, 1), 0, top)
    return jnp.take_along_axis(table, (jnp.arange(top)[None, :] + offset_by) % top, axis=1)


def load_shares(count, total, limit, slope, full):
    loads = [(1 << 20) // math.isqrt(rank ** slope) + 1 for rank in range(1, count + 1)]
    largest = limit if full else min(limit, max(-(-total // count), total * loads[0] // sum(loads)))
    least = 1 if total - largest >= count - 1 else 0
    holding, rest = [largest] + [least] * (count - 1), total - largest - least * (count - 1)
    while rest > 0:
        movable = [i for i in range(1, count) if holding[i] < largest] or [i for i in range(1, count) if holding[i] < limit]
        pool, remaining = sum([loads[i] for i in movable]), rest
        for i in movable:
            addition = min(limit - holding[i], max(1, remaining * loads[i] // pool), rest)
            holding[i] = holding[i] + addition
            rest = rest - addition
    return np.array(holding)


def normal_values(own_key, shape, scale, reach, shards=(), kind=jnp.bfloat16):
    level = block_levels(own_key, shape, shards, -0.22, 0.18) if shards else 1.0
    values = jax.random.normal(own_key, shape, jnp.float32) * scale * level
    return jnp.minimum(jnp.maximum(values, -reach), reach).astype(kind)


def setup_inputs(seed: int = 0) -> dict:
    seeds = jax.random.split(jax.random.key(seed), 6)
    tokens = draw_tokens(jax.random.fold_in(seeds[5], 71), 0)
    routes_keys = jax.random.split(jax.random.fold_in(seeds[1], 1), TOKENS // TOK_DEV)
    routes_turns = jax.random.permutation(jax.random.fold_in(seeds[1], 3), TOKENS // TOK_DEV)
    routes = jax.vmap(lambda own, number: assign_block(jax.random.fold_in(seeds[1], 2), own, number, TOK_DEV, MEMS, TOP, CAP, 1))(routes_keys, routes_turns).reshape((TOKENS, TOP))
    router = normal_values(seeds[2], (D, MEMS), D ** -0.5, 0.1875)
    mem_weight = normal_values(seeds[3], (MEMS, D, 3 * HEADS * HDIM), D ** -0.5, 0.1875, ((0, 16),))
    win_weight = draw_win_weight(jax.random.fold_in(seeds[5], 71), 0)
    return dict(tokens=tokens, routes=routes, router=router, mem_weight=mem_weight, win_weight=win_weight)


norm_eps = 1e-06

def slot_table(route_rows, mems):
    matches = (route_rows[:, :, None] == jnp.arange(mems, dtype=jnp.int32)[None, None, :]).astype(jnp.int32)
    flat = matches.reshape(-1, mems)
    earlier = jnp.cumsum(flat, axis=0) - flat
    return lax.optimization_barrier(jnp.sum(earlier * flat, axis=1)).reshape(route_rows.shape).astype(jnp.int32)

def memory_local(slot_rows, positions, weight):
    projected = jnp.dot(slot_rows, weight, preferred_element_type=jnp.float32).astype(jnp.bfloat16)
    width = HEADS * HDIM
    causal = positions[None, :] <= positions[:, None]
    intra_list = []
    state_list = []
    for head_index in range(HEADS):
        column_start = head_index * HDIM
        queries = projected[:, column_start:column_start + HDIM]
        key_rows = projected[:, width + column_start:width + column_start + HDIM]
        value_rows = projected[:, 2 * width + column_start:2 * width + column_start + HDIM]
        scores = lax.dot_general(queries, key_rows, (((1,), (1,)), ((), ())), preferred_element_type=jnp.float32)
        weights_low = jnp.where(causal, scores, 0.0).astype(jnp.bfloat16)
        intra_list.append(jnp.dot(weights_low, value_rows, preferred_element_type=jnp.float32))
        state_list.append(lax.dot_general(key_rows, value_rows, (((0,), (0,)), ((), ())), preferred_element_type=jnp.float32))
    return (projected[:, :width], jnp.stack(intra_list), jnp.stack(state_list))

def memory_finish(queries, intra, prefix):
    outputs = []
    for head_index in range(HEADS):
        column_start = head_index * HDIM
        inter = jnp.dot(queries[:, column_start:column_start + HDIM], prefix[head_index].astype(jnp.bfloat16), preferred_element_type=jnp.float32)
        summed = intra[head_index] + inter
        factor = lax.rsqrt(lax.optimization_barrier(jnp.mean(summed * summed, axis=-1, keepdims=True)) + norm_eps)
        outputs.append(summed * factor)
    return jnp.concatenate(outputs, axis=-1).astype(jnp.bfloat16)

def window_attend(queries, key_rows, value_rows, first_pos, count):
    distance = jnp.arange(count, dtype=jnp.int32)[:, None] + 2 * count - jnp.arange(3 * count, dtype=jnp.int32)[None, :]
    key_pos = first_pos - 2 * count + jnp.arange(3 * count, dtype=jnp.int32)
    allowed = (distance >= 0) & (distance < WINDOW) & (key_pos[None, :] >= 0)
    outputs = []
    for head_index in range(HEADS):
        column_start = head_index * HDIM
        scores = lax.dot_general(queries[:, column_start:column_start + HDIM], key_rows[:, column_start:column_start + HDIM], (((1,), (1,)), ((), ())), preferred_element_type=jnp.float32) * HDIM ** (-0.5)
        masked = jnp.where(allowed, scores, -1e+30)
        highest = lax.optimization_barrier(jnp.max(masked, axis=-1, keepdims=True))
        expo = jnp.exp(masked - highest)
        probs = (expo / lax.optimization_barrier(jnp.sum(expo, axis=-1, keepdims=True))).astype(jnp.bfloat16)
        outputs.append(jnp.dot(probs, value_rows[:, column_start:column_start + HDIM], preferred_element_type=jnp.float32))
    return jnp.concatenate(outputs, axis=-1)

def reference(tokens, routes, router, mem_weight, win_weight):
    block_rows = N_MEM * TOK_DEV
    width = HEADS * HDIM
    logits = jnp.dot(tokens, router, preferred_element_type=jnp.float32)
    chosen = jnp.take_along_axis(logits, routes, axis=1)
    gate_first = jax.nn.sigmoid(chosen[:, 0] - chosen[:, 1])
    sources = jnp.arange(N_MEM, dtype=jnp.int32)
    row_ids = jnp.broadcast_to(jnp.arange(TOK_DEV, dtype=jnp.int32)[:, None], (TOK_DEV, TOP))

    def block_step(states, block_index):
        rows = lax.dynamic_slice_in_dim(tokens, block_index * block_rows, block_rows, 0).reshape(N_MEM, TOK_DEV, D)
        block_routes = lax.dynamic_slice_in_dim(routes, block_index * block_rows, block_rows, 0).reshape(N_MEM, TOK_DEV, TOP)
        gates = lax.dynamic_slice_in_dim(gate_first, block_index * block_rows, block_rows, 0).reshape(N_MEM, TOK_DEV)
        slots = jax.vmap(lambda group_routes: slot_table(group_routes, MEMS))(block_routes)

        def owner(packed):
            memory, weight, prefix = packed
            target = jnp.where(block_routes == memory, slots, CAP)

            def fill(token_rows, places):
                values = jnp.broadcast_to(token_rows[:, None, :], (TOK_DEV, TOP, D))
                dispatch = jnp.zeros((CAP, D), jnp.bfloat16).at[places].set(values, mode='drop')
                found = jnp.full((CAP,), -1, jnp.int32).at[places].set(row_ids, mode='drop')
                return (dispatch, found)
            dispatch, found = jax.vmap(fill)(rows, target)
            positions = (sources[:, None] * TOK_DEV + found).reshape(-1)
            queries, intra, state = memory_local(dispatch.reshape(N_MEM * CAP, D), positions, weight)
            return (memory_finish(queries, intra, prefix).reshape(N_MEM, CAP, width), state)
        outputs, block_states = lax.map(owner, (jnp.arange(MEMS, dtype=jnp.int32), mem_weight, states))
        picked = outputs[block_routes, sources[:, None, None], slots].astype(jnp.float32)
        combined = gates[..., None] * picked[:, :, 0] + (1.0 - gates)[..., None] * picked[:, :, 1]
        return (states + block_states, combined.reshape(block_rows, width))
    start_states = jnp.zeros((MEMS, HEADS, HDIM, HDIM), jnp.float32)
    _, memory_part = lax.scan(block_step, start_states, jnp.arange(N_CTX, dtype=jnp.int32))
    memory_part = memory_part.reshape(TOKENS, width)
    projected = jnp.dot(tokens, win_weight, preferred_element_type=jnp.float32).astype(jnp.bfloat16)
    padded = jnp.concatenate([jnp.zeros((2 * TOK_DEV, 3 * width), jnp.bfloat16), projected], axis=0)

    def window_block(block_index):
        own = lax.dynamic_slice_in_dim(projected, block_index * TOK_DEV, TOK_DEV, 0)
        keys = lax.dynamic_slice_in_dim(padded, block_index * TOK_DEV, 3 * TOK_DEV, 0)
        return window_attend(own[:, :width], keys[:, width:2 * width], keys[:, 2 * width:], block_index * TOK_DEV, TOK_DEV)
    window_part = lax.map(window_block, jnp.arange(TOKENS // TOK_DEV, dtype=jnp.int32)).reshape(TOKENS, width)
    return (memory_part + window_part).astype(jnp.bfloat16)
```

```python
import functools

import jax
import jax.numpy as jnp
from jax import lax
from jax.experimental import pallas as pl
from jax.experimental.pallas import tpu as pltpu
from jax.sharding import PartitionSpec as P

MESH = pl.DeviceIdType.MESH
HEADS = 4
HDIM = 128
WIDTH = HEADS * HDIM
WINDOW = 512
TOK = 256
MEMS = 16
CAP = 48
ROWS = MEMS * CAP
DEPTH = 1024
COLS = 3 * WIDTH
CHIPS = 16
WIN_TILES = COLS // 128
norm_eps = 1e-06
bf16 = jnp.bfloat16
f32 = jnp.float32


def mm(a, b):
    return jnp.dot(a, b, preferred_element_type=f32)


def mm_nt(a, b):
    return lax.dot_general(a, b, (((1,), (1,)), ((), ())), preferred_element_type=f32)


def mm_tn(a, b):
    return lax.dot_general(a, b, (((0,), (0,)), ((), ())), preferred_element_type=f32)


def remote(src, dst, send, recv, device):
    return pltpu.make_async_remote_copy(
        src_ref=src, dst_ref=dst, send_sem=send, recv_sem=recv, device_id=device, device_id_type=MESH
    )


def cols(start, size=128):
    return pl.ds(pl.multiple_of(start, 128), size)


def rows_of(j, size=CAP):
    return pl.ds(pl.multiple_of(j * size, 16), size)


def loop(low, high, body):
    def step(n, carry):
        body(n)
        return carry

    lax.fori_loop(low, high, step, 0)


def kernel(
    tok, routes, router, w_hbm, win, out,
    pick0, pick1, sbuf, rbuf, wmem, wz, wwin, proj, intra, winq, kv,
    st_own, st_part, st_send, st_all, pre_send, pre_part, pre, fbuf, ret, wout, gcol,
    s_disp, r_disp, s_ret, r_ret, s_wz, r_wz, s_wp, r_wp, s_st, r_st, one_s, one_r, local,
):
    ctx = lax.axis_index("ctx")
    me = lax.axis_index("mem")
    chip = ctx // 2
    core = ctx % 2
    blk = ctx
    seq = blk * MEMS + me

    def member(j):
        return {"ctx": ctx, "mem": j}

    def peer(j):
        return {"ctx": 2 * j + core, "mem": me}

    def at_seq(n):
        n = (n + 32 * MEMS) % (32 * MEMS)
        return {"ctx": n // MEMS, "mem": n % MEMS}

    partner = {"ctx": 2 * chip + 1 - core, "mem": me}

    w_copy = pltpu.make_async_copy(w_hbm.at[0], wmem, local.at[0])
    w_copy.start()

    barrier = pltpu.get_barrier_semaphore()

    def greet(off):
        pl.semaphore_signal(barrier, inc=1, device_id=member((me + off) % MEMS), device_id_type=MESH)
        pl.semaphore_signal(barrier, inc=1, device_id=peer((chip + off) % CHIPS), device_id_type=MESH)

    loop(1, 16, greet)
    pl.semaphore_signal(barrier, inc=1, device_id=partner, device_id_type=MESH)
    for off in (-2, -1, 1, 2):
        pl.semaphore_signal(barrier, inc=1, device_id=at_seq(seq + off), device_id_type=MESH)

    first, second = routes[0:1, :], routes[1:2, :]
    mem_ids = lax.broadcasted_iota(jnp.int32, (MEMS, TOK), 0)
    match0 = jnp.where(mem_ids == first, 1.0, 0.0).astype(f32)
    match1 = jnp.where(mem_ids == second, 1.0, 0.0).astype(f32)
    earlier = jnp.where(
        lax.broadcasted_iota(jnp.int32, (TOK, TOK), 0) < lax.broadcasted_iota(jnp.int32, (TOK, TOK), 1), 1.0, 0.0
    ).astype(bf16)
    counts = mm((match0 + match1).astype(bf16), earlier)
    slot0 = jnp.sum(match0 * counts, axis=0, keepdims=True).astype(jnp.int32)
    slot1 = jnp.sum(match1 * counts, axis=0, keepdims=True).astype(jnp.int32)
    row_ids = lax.broadcasted_iota(jnp.int32, (ROWS, TOK), 0)
    is0 = jnp.where(row_ids == first * CAP + slot0, 1.0, 0.0).astype(f32)
    is1 = jnp.where(row_ids == second * CAP + slot1, 1.0, 0.0).astype(f32)
    pick0[...] = is0.astype(bf16)
    pick1[...] = is1.astype(bf16)
    picked = (is0 + is1).astype(bf16)
    for n in range(2):
        sbuf[:, n * 512 : (n + 1) * 512] = mm(picked, tok[:, n * 512 : (n + 1) * 512]).astype(bf16)

    logits = mm_nt(router[...], tok[...])
    diff = jnp.sum((match0 - match1) * logits, axis=0, keepdims=True)
    gate = jax.nn.sigmoid(diff)
    gcol[...] = jnp.transpose(jnp.broadcast_to(gate, (128, TOK)))

    pl.semaphore_wait(barrier, 15 + 15 + 1 + 4)

    half = pl.ds(pl.multiple_of(core * 32, 32), 32)

    def wz_copy(j, slot, device):
        return remote(win.at[half, cols(chip * 128)], wz.at[slot], s_wz.at[j], r_wz.at[slot], device)

    @pl.when(chip < WIN_TILES)
    def _():
        def send(off):
            j = (me + off) % MEMS
            wz_copy(j, me, member(j)).start()

        loop(1, 16, send)
        pltpu.make_async_copy(win.at[half, cols(chip * 128)], wz.at[me], local.at[1]).start()

    def disp_copy(j, slot, device):
        return remote(sbuf.at[rows_of(j)], rbuf.at[rows_of(slot)], s_disp.at[j], r_disp.at[slot], device)

    def send_rows(n):
        near = 8 - (n + 1) // 2
        off = jnp.where(n % 2 == 0, near, MEMS - near)
        j = (me + off) % MEMS
        disp_copy(j, me, member(j)).start()

    loop(0, 15, send_rows)
    own_rows = pltpu.make_async_copy(sbuf.at[rows_of(me)], rbuf.at[rows_of(me)], local.at[2])
    own_rows.start()

    def wp_block(j, b):
        return wwin.at[:, pl.ds(pl.multiple_of(b * 32, 32), 32), cols(j * 128)]

    @pl.when(chip < WIN_TILES)
    def _():
        def arrive(off):
            j = (me + off) % MEMS
            wz_copy(j, j, member(j)).wait_recv()

        loop(1, 16, arrive)
        pltpu.make_async_copy(win.at[half, cols(chip * 128)], wz.at[me], local.at[1]).wait()

        def send(off):
            j = (chip + off) % CHIPS
            remote(wz, wp_block(chip, core), s_wp.at[j], r_wp.at[chip], peer(j)).start()

        loop(1, 16, send)
        pltpu.make_async_copy(wz, wp_block(chip, core), local.at[1]).start()

    def wp_arrive(j):
        @pl.when(j != chip)
        def _():
            remote(wz, wp_block(j, core), s_wp.at[j], r_wp.at[j], partner).wait_recv()

        @pl.when(j == chip)
        def _():
            pltpu.make_async_copy(wz, wp_block(j, core), local.at[1]).wait()

    loop(0, WIN_TILES, wp_arrive)
    wc_copy = remote(wwin.at[:, half, :], wwin.at[:, half, :], one_s.at[0], one_r.at[0], partner)
    wc_copy.start()
    wc_copy.wait_recv()

    def win_project(n):
        w = wwin[:, :, cols(n * 256, 256)].reshape(DEPTH, 256)
        res = mm(tok[...], w).astype(bf16)

        @pl.when(n < 2)
        def _():
            winq[:, cols(n * 256, 256)] = res

        @pl.when(n >= 2)
        def _():
            kv[pl.ds(2 * TOK, TOK), cols((n - 2) * 256, 256)] = res

    loop(0, 6, win_project)

    w_copy.wait()

    def project(g):
        def arrive(k):
            j = 4 * g + k

            @pl.when(j != me)
            def _():
                disp_copy(j, j, partner).wait_recv()

            @pl.when(j == me)
            def _():
                own_rows.wait()

        loop(0, 4, arrive)

        def tile(n):
            proj[rows_of(g, 192), cols(n * 512, 512)] = mm(rbuf[rows_of(g, 192), :], wmem[:, cols(n * 512, 512)]).astype(
                bf16
            )

        loop(0, 3, tile)

    loop(0, 4, project)

    def kv_copy(n):
        return remote(
            kv.at[pl.ds(2 * TOK, TOK)],
            kv.at[pl.ds((2 - n) * TOK, TOK)],
            one_s.at[n],
            one_r.at[n],
            at_seq(seq + n),
        )

    kv_copy(1).start()
    kv_copy(2).start()

    def state(h):
        st_own[h] = mm_tn(proj[:, cols(WIDTH + h * HDIM)], proj[:, cols(2 * WIDTH + h * HDIM)])

    loop(0, HEADS, state)
    st_copy = remote(st_own, st_part, one_s.at[3], one_r.at[3], partner)
    st_copy.start()

    def attend(h):
        q = proj[:, cols(h * HDIM)]
        k = proj[:, cols(WIDTH + h * HDIM)]
        v = proj[:, cols(2 * WIDTH + h * HDIM)]
        keep = lax.broadcasted_iota(jnp.int32, (256, 256), 1) <= lax.broadcasted_iota(jnp.int32, (256, 256), 0)
        for b in range(3):
            lo, hi = b * 256, (b + 1) * 256
            scores = jnp.where(keep, mm_nt(q[lo:hi], k[lo:hi]), 0.0).astype(bf16)
            total = mm(scores, v[lo:hi])
            if b:
                total = total + mm(mm_nt(q[lo:hi], k[:lo]).astype(bf16), v[:lo])
            intra[lo:hi, cols(h * HDIM)] = total

    st_copy.wait()
    mine = pl.ds(2 * core, 2)
    st_send[...] = (st_own[mine] + st_part[mine]).astype(bf16)

    def st_copy_of(j, slot, device):
        return remote(st_send, st_all.at[slot], s_st.at[j], r_st.at[slot], device)

    def st_out(j):
        st_copy_of(j, chip, peer(j)).start()

    loop(chip + 1, CHIPS, st_out)
    loop(0, HEADS, attend)
    pre_send[...] = jnp.zeros_like(pre_send)

    def st_in(j):
        st_copy_of(j, j, partner).wait_recv()
        pre_send[...] += st_all[j].astype(f32)

    loop(0, chip, st_in)
    pre_copy = remote(pre_send, pre_part, one_s.at[4], one_r.at[4], partner)
    pre_copy.start()
    pre_copy.wait_recv()

    for h in range(HEADS):
        lower = core == h // 2

        @pl.when(lower)
        def _():
            st_own[h] = pre_send[h % 2]

        @pl.when(jnp.logical_not(lower))
        def _():
            st_own[h] = pre_part[h % 2]

    @pl.when(core == 0)
    def _():
        pre[...] = st_own[...].astype(bf16)

    @pl.when(core == 1)
    def _():
        pre[...] = (st_own[...] + st_part[...]).astype(bf16)

    def finish(h):
        summed = intra[:, cols(h * HDIM)] + mm(proj[:, cols(h * HDIM)], pre[h])
        factor = lax.rsqrt(jnp.mean(summed * summed, axis=-1, keepdims=True) + norm_eps)
        fbuf[:, cols(h * HDIM)] = (summed * factor).astype(bf16)

    loop(0, HEADS, finish)

    def ret_copy(j, slot, device):
        return remote(fbuf.at[rows_of(j)], ret.at[rows_of(slot)], s_ret.at[j], r_ret.at[slot], device)

    def send_back(n):
        near = 8 - (n + 1) // 2
        off = jnp.where(n % 2 == 0, near, MEMS - near)
        j = (me + off) % MEMS
        ret_copy(j, me, member(j)).start()

    loop(0, 15, send_back)
    own_ret = pltpu.make_async_copy(fbuf.at[rows_of(me)], ret.at[rows_of(me)], local.at[3])
    own_ret.start()

    kv_copy(1).wait_recv()
    kv_copy(2).wait_recv()
    first_pos = seq * TOK

    def window(h):
        for b in range(2):
            lo = b * 128
            q = winq[lo : lo + 128, cols(h * HDIM)]
            k = kv[lo : lo + 640, cols(h * HDIM)]
            v = kv[lo : lo + 640, cols(WIDTH + h * HDIM)]
            scores = mm_nt(q, k) * HDIM ** (-0.5)
            key = lax.broadcasted_iota(jnp.int32, (128, 640), 1)
            distance = lax.broadcasted_iota(jnp.int32, (128, 640), 0) + 2 * TOK - key
            allowed = (distance >= 0) & (distance < WINDOW) & (key + lo + first_pos - 2 * TOK >= 0)
            masked = jnp.where(allowed, scores, -1e30)
            expo = jnp.exp(masked - jnp.max(masked, axis=-1, keepdims=True))
            probs = (expo / jnp.sum(expo, axis=-1, keepdims=True)).astype(bf16)
            wout[lo : lo + 128, cols(h * HDIM)] = mm(probs, v)

    loop(0, HEADS, window)

    def ret_in(off):
        j = (me + off) % MEMS
        ret_copy(j, j, member(j)).wait_recv()

    loop(1, 16, ret_in)
    own_ret.wait()

    def combine(h):
        res = ret[:, cols(h * HDIM)]
        g = gcol[...]
        part = g * mm_tn(pick0[...], res) + (1.0 - g) * mm_tn(pick1[...], res)
        out[:, cols(h * HDIM)] = (part + wout[:, cols(h * HDIM)]).astype(bf16)

    loop(0, HEADS, combine)

    def left(off):
        j = (me + off) % MEMS
        disp_copy(j, me, member(j)).wait_send()
        ret_copy(j, me, member(j)).wait_send()

        @pl.when(chip < WIN_TILES)
        def _():
            wz_copy(j, me, member(j)).wait_send()
            i = (chip + off) % CHIPS
            remote(wz, wp_block(chip, core), s_wp.at[i], r_wp.at[chip], peer(i)).wait_send()

    loop(1, 16, left)

    def st_left(j):
        st_copy_of(j, chip, peer(j)).wait_send()

    loop(chip + 1, CHIPS, st_left)
    wc_copy.wait_send()
    kv_copy(1).wait_send()
    kv_copy(2).wait_send()
    pre_copy.wait_send()


def shards(tokens, routes, router, mem_weight, win_weight):
    vmem = pl.BlockSpec(memory_space=pltpu.VMEM)
    dma = pltpu.SemaphoreType.DMA
    return pl.pallas_call(
        kernel,
        out_shape=jax.ShapeDtypeStruct((TOK, WIDTH), bf16),
        in_specs=[vmem, vmem, vmem, pl.BlockSpec(memory_space=pl.ANY), vmem],
        out_specs=vmem,
        scratch_shapes=[
            pltpu.VMEM((ROWS, TOK), bf16),
            pltpu.VMEM((ROWS, TOK), bf16),
            pltpu.VMEM((ROWS, DEPTH), bf16),
            pltpu.VMEM((ROWS, DEPTH), bf16),
            pltpu.VMEM((DEPTH, COLS), bf16),
            pltpu.VMEM((MEMS, 32, 128), bf16),
            pltpu.VMEM((MEMS, 64, COLS), bf16),
            pltpu.VMEM((ROWS, COLS), bf16),
            pltpu.VMEM((ROWS, WIDTH), f32),
            pltpu.VMEM((TOK, WIDTH), bf16),
            pltpu.VMEM((3 * TOK, 2 * WIDTH), bf16),
            pltpu.VMEM((HEADS, HDIM, HDIM), f32),
            pltpu.VMEM((HEADS, HDIM, HDIM), f32),
            pltpu.VMEM((2, HDIM, HDIM), bf16),
            pltpu.VMEM((CHIPS, 2, HDIM, HDIM), bf16),
            pltpu.VMEM((2, HDIM, HDIM), f32),
            pltpu.VMEM((2, HDIM, HDIM), f32),
            pltpu.VMEM((HEADS, HDIM, HDIM), bf16),
            pltpu.VMEM((ROWS, WIDTH), bf16),
            pltpu.VMEM((ROWS, WIDTH), bf16),
            pltpu.VMEM((TOK, WIDTH), f32),
            pltpu.VMEM((TOK, 128), f32),
        ]
        + [dma((16,))] * 10
        + [dma((5,)), dma((5,)), dma((4,))],
        compiler_params=pltpu.CompilerParams(
            collective_id=0, has_side_effects=True, vmem_limit_bytes=56 * 1024 * 1024
        ),
    )(tokens, routes.T, router.T, mem_weight, win_weight)


def solution(mesh):
    return jax.shard_map(
        shards,
        mesh=mesh,
        in_specs=(
            P(("ctx", "mem"), None),
            P(("ctx", "mem"), None),
            P(),
            P("mem", None, None),
            P("mem", None),
        ),
        out_specs=P(("ctx", "mem"), None),
        check_vma=False,
    )
```

```python
import functools

import jax
import jax.numpy as jnp
from jax import lax
from jax.experimental import pallas as pl
from jax.experimental.pallas import tpu as pltpu
from jax.sharding import PartitionSpec as P

MESH = pl.DeviceIdType.MESH
HEADS = 4
HDIM = 128
WIDTH = HEADS * HDIM
WINDOW = 512
TOK = 256
MEMS = 16
CAP = 48
ROWS = MEMS * CAP
DEPTH = 1024
COLS = 3 * WIDTH
CHIPS = 16
WIN_TILES = COLS // 128
norm_eps = 1e-06
bf16 = jnp.bfloat16
f32 = jnp.float32


def mm(a, b):
    return jnp.dot(a, b, preferred_element_type=f32)


def mm_nt(a, b):
    return lax.dot_general(a, b, (((1,), (1,)), ((), ())), preferred_element_type=f32)


def mm_tn(a, b):
    return lax.dot_general(a, b, (((0,), (0,)), ((), ())), preferred_element_type=f32)


def remote(src, dst, send, recv, device):
    return pltpu.make_async_remote_copy(
        src_ref=src, dst_ref=dst, send_sem=send, recv_sem=recv, device_id=device, device_id_type=MESH
    )


def cols(start, size=128):
    return pl.ds(pl.multiple_of(start, 128), size)


def rows_of(j, size=CAP):
    return pl.ds(pl.multiple_of(j * size, 16), size)


def loop(low, high, body):
    def step(n, carry):
        body(n)
        return carry

    lax.fori_loop(low, high, step, 0)


def kernel(
    tok, routes, router, w_hbm, win, out,
    near, slots_in, pick, pick0, pick1, sbuf, rbuf, wmem, wz, wwin, proj, intra, winq, kv, kvx,
    st_own, st_part, st_send, st_all, pre_send, pre_part, pre, fbuf, ret, wout, gcol, slots,
    s_chain, r_chain, s_slot, r_slot, s_disp, r_disp, r_far, s_ret, r_ret, s_wz, r_wz, s_wp, r_wp, s_st, r_st,
    one_s, one_r, l_ret, local,
):
    ctx = lax.axis_index("ctx")
    me = lax.axis_index("mem")
    chip = ctx // 2
    core = ctx % 2
    seq = ctx * MEMS + me

    def member(j):
        return {"ctx": ctx, "mem": j}

    def peer(j):
        return {"ctx": 2 * j + core, "mem": me}

    def wrap(n):
        return (n + 32) % 16

    partner = {"ctx": 2 * chip + 1 - core, "mem": me}
    after = {"ctx": (ctx + 1) % 32, "mem": me}
    before = {"ctx": (ctx + 31) % 32, "mem": me}

    w_copy = pltpu.make_async_copy(w_hbm.at[0], wmem, local.at[0])
    w_copy.start()

    barrier = pltpu.get_barrier_semaphore()

    def greet(off):
        pl.semaphore_signal(barrier, inc=1, device_id=member(wrap(me + off)), device_id_type=MESH)
        pl.semaphore_signal(barrier, inc=1, device_id=peer(wrap(chip + off)), device_id_type=MESH)

    loop(1, 16, greet)
    for device in (partner, after, before):
        pl.semaphore_signal(barrier, inc=1, device_id=device, device_id_type=MESH)

    first, second = routes[0:1, :], routes[1:2, :]
    mem_ids = lax.broadcasted_iota(jnp.int32, (MEMS, TOK), 0)
    match0 = jnp.where(mem_ids == first, 1.0, 0.0).astype(f32)
    match1 = jnp.where(mem_ids == second, 1.0, 0.0).astype(f32)
    earlier = jnp.where(
        lax.broadcasted_iota(jnp.int32, (TOK, TOK), 0) < lax.broadcasted_iota(jnp.int32, (TOK, TOK), 1), 1.0, 0.0
    ).astype(bf16)
    counts = mm((match0 + match1).astype(bf16), earlier)
    slot0 = jnp.sum(match0 * counts, axis=0, keepdims=True).astype(jnp.int32)
    slot1 = jnp.sum(match1 * counts, axis=0, keepdims=True).astype(jnp.int32)
    slots[0:1, :] = first * CAP + slot0
    slots[1:2, :] = second * CAP + slot1

    def chosen(table, memory, size=CAP, skip=0):
        ids = lax.broadcasted_iota(jnp.int32, (size, TOK), 0) + (memory * CAP + skip)
        return jnp.where((ids == table[0:1, :]) | (ids == table[1:2, :]), 1.0, 0.0).astype(bf16)

    own_pick = chosen(slots, me)
    rbuf[rows_of(me), :] = mm(own_pick, tok[...]).astype(bf16)

    pl.semaphore_wait(barrier, 15 + 15 + 1 + 2)

    ways = (1, -1)

    def chain(d, hop, k):
        part = cols(k * 256, 256)
        src = tok.at[:, part] if hop == 0 else near.at[d, 0, :, part]
        at = (2 * d + hop) * 4 + k
        return remote(src, near.at[d, hop, :, part], s_chain.at[at], r_chain.at[at], member(wrap(me + ways[d])))

    def slot_chain(d, hop):
        src = slots if hop == 0 else slots_in.at[d, 0]
        at = 2 * d + hop
        return remote(src, slots_in.at[d, hop], s_slot.at[at], r_slot.at[at], member(wrap(me + ways[d])))

    for d in range(2):
        slot_chain(d, 0).start()

    def first_hop(k):
        for d in range(2):
            chain(d, 0, k).start()

    loop(0, 4, first_hop)

    half = pl.ds(pl.multiple_of(core * 32, 32), 32)

    def wz_copy(j, slot, device):
        return remote(win.at[half, cols(chip * 128)], wz.at[slot], s_wz.at[j], r_wz.at[slot], device)

    @pl.when(chip < WIN_TILES)
    def _():
        def send(off):
            j = wrap(me + off)
            wz_copy(j, me, member(j)).start()

        loop(1, 16, send)
        pltpu.make_async_copy(win.at[half, cols(chip * 128)], wz.at[me], local.at[1]).start()

    far = (32, 16)

    def disp_copy(d, e, k):
        part = cols(k * 256, 256)
        size = CAP if e < 5 else far[d]
        skip = far[0] if e == 5 and d else 0
        slot = wrap(me - 2 * ways[d])
        target = pl.ds(pl.multiple_of(slot * CAP + skip, 16), size)
        recv = r_far.at[k] if e == 5 and d else r_disp.at[16 * k + slot]
        return remote(
            sbuf.at[d, e * CAP : e * CAP + size, part],
            rbuf.at[target, part],
            s_disp.at[(d * 6 + e) * 4 + k],
            recv,
            member(wrap(me + ways[d] * (1 + e))),
        )

    def second_hop(k):
        for d in range(2):
            chain(d, 0, k).wait_recv()
            chain(d, 1, k).start()

    def relay(k):
        part = cols(k * 256, 256)
        for d in range(2):
            chain(d, 1, k).wait_recv()
            sbuf[d, :, part] = mm(pick[d], near[d, 1, :, part]).astype(bf16)
            for e in range(5, -1, -1):
                disp_copy(d, e, k).start()

    for d in range(2):
        slot_chain(d, 0).wait_recv()
        slot_chain(d, 1).start()
    loop(0, 2, second_hop)
    def wp_block(j, b):
        return wwin.at[:, pl.ds(pl.multiple_of(b * 32, 32), 32), cols(j * 128)]

    @pl.when(chip < WIN_TILES)
    def _():
        def arrive(off):
            j = wrap(me + off)
            wz_copy(j, j, member(j)).wait_recv()

        loop(1, 16, arrive)
        pltpu.make_async_copy(win.at[half, cols(chip * 128)], wz.at[me], local.at[1]).wait()

        def send(off):
            j = wrap(chip + off)
            remote(wz, wp_block(chip, core), s_wp.at[j], r_wp.at[chip], peer(j)).start()

        loop(1, 16, send)
        pltpu.make_async_copy(wz, wp_block(chip, core), local.at[1]).start()

    for d in range(2):
        slot_chain(d, 1).wait_recv()
        for e in range(6):
            size = CAP if e < 5 else far[d]
            skip = far[0] if e == 5 and d else 0
            pick[d, e * CAP : e * CAP + size] = chosen(slots_in[d, 1], wrap(me + ways[d] * (1 + e)), size, skip)
        if d:
            pick[d, 5 * CAP + far[1] : 5 * CAP + far[0]] = jnp.zeros((far[0] - far[1], TOK), bf16)
    relay(0)
    second_hop(2)
    relay(1)
    second_hop(3)
    loop(2, 4, relay)

    for d in range(2):
        for hop in range(2):
            mine = chosen(slots_in[d, hop], me)
            rbuf[rows_of(wrap(me - ways[d] * (hop + 1))), :] = mm(mine, near[d, hop]).astype(bf16)

    logits = mm_nt(router[...], tok[...])
    diff = jnp.sum((match0 - match1) * logits, axis=0, keepdims=True)
    gate = jax.nn.sigmoid(diff)
    gcol[...] = jnp.transpose(jnp.broadcast_to(gate, (128, TOK)))
    row_ids = lax.broadcasted_iota(jnp.int32, (ROWS, TOK), 0)
    pick0[...] = jnp.where(row_ids == slots[0:1, :], 1.0, 0.0).astype(bf16)
    pick1[...] = jnp.where(row_ids == slots[1:2, :], 1.0, 0.0).astype(bf16)

    def wp_arrive(j):
        @pl.when(j != chip)
        def _():
            remote(wz, wp_block(j, core), s_wp.at[j], r_wp.at[j], partner).wait_recv()

        @pl.when(j == chip)
        def _():
            pltpu.make_async_copy(wz, wp_block(j, core), local.at[1]).wait()

    loop(0, WIN_TILES, wp_arrive)
    wc_copy = remote(wwin.at[:, half, :], wwin.at[:, half, :], one_s.at[0], one_r.at[0], partner)
    wc_copy.start()
    wc_copy.wait_recv()

    def win_block(n):
        return wwin[:, :, cols(n * 256, 256)].reshape(DEPTH, 256)

    def win_query(n):
        winq[:, cols(n * 256, 256)] = mm(tok[...], win_block(n)).astype(bf16)

    loop(0, 2, win_query)

    crosses = (me <= 1, me == 0)

    def win_keys(n):
        w = win_block(n + 2)
        at = cols(n * 256, 256)
        kv[2 * TOK : 3 * TOK, at] = mm(tok[...], w).astype(bf16)
        for g in range(2):
            res = mm(near[0, 1 - g], w).astype(bf16)

            @pl.when(crosses[g])
            def _():
                kvx[g * TOK : (g + 1) * TOK, at] = res

            @pl.when(jnp.logical_not(crosses[g]))
            def _():
                kv[g * TOK : (g + 1) * TOK, at] = res

    loop(0, 4, win_keys)

    def kv_copy(g):
        rows = pl.ds(g * TOK, TOK)
        return remote(kvx.at[rows], kv.at[rows], one_s.at[1 + g], one_r.at[1 + g], after)

    for g in range(2):

        @pl.when(crosses[g])
        def _():
            kv_copy(g).start()

    w_copy.wait()

    def arrived(dist, k):
        j = wrap(me - dist)
        part = cols(k * 256, 256)
        return remote(
            rbuf.at[rows_of(j), part], rbuf.at[rows_of(j), part], s_disp.at[0], r_disp.at[16 * k + j], partner
        )

    def half_arrived(d, k):
        j = wrap(me + 8)
        part = cols(k * 256, 256)
        target = pl.ds(pl.multiple_of(j * CAP + (far[0] if d else 0), 16), far[d])
        sem = r_far.at[k] if d else r_disp.at[16 * k + j]
        return remote(rbuf.at[target, part], rbuf.at[target, part], s_disp.at[0], sem, partner)

    def all_arrived(k):
        def one(dist):
            arrived(dist, k).wait_recv()
            arrived(-dist, k).wait_recv()

        loop(3, 8, one)
        half_arrived(0, k).wait_recv()
        half_arrived(1, k).wait_recv()

    loop(0, 4, all_arrived)

    def project(n):
        def tile(g):
            proj[rows_of(g, 256), cols(n * 256, 256)] = mm(rbuf[rows_of(g, 256), :], wmem[:, cols(n * 256, 256)]).astype(
                bf16
            )

        loop(0, 3, tile)

    loop(2, 6, project)

    def state(h):
        st_own[h] = mm_tn(proj[:, cols(WIDTH + h * HDIM)], proj[:, cols(2 * WIDTH + h * HDIM)])

    loop(0, HEADS, state)
    st_copy = remote(st_own, st_part, one_s.at[3], one_r.at[3], partner)
    st_copy.start()
    loop(0, 2, project)
    st_copy.wait()
    mine = pl.ds(2 * core, 2)
    st_send[...] = (st_own[mine] + st_part[mine]).astype(bf16)

    def st_copy_of(j, slot, device):
        return remote(st_send, st_all.at[slot], s_st.at[j], r_st.at[slot], device)

    loop(chip + 1, CHIPS, lambda j: st_copy_of(j, chip, peer(j)).start())

    def attend(h):
        q = proj[:, cols(h * HDIM)]
        k = proj[:, cols(WIDTH + h * HDIM)]
        v = proj[:, cols(2 * WIDTH + h * HDIM)]
        keep = lax.broadcasted_iota(jnp.int32, (256, 256), 1) <= lax.broadcasted_iota(jnp.int32, (256, 256), 0)
        for b in range(3):
            lo, hi = b * 256, (b + 1) * 256
            scores = jnp.where(keep, mm_nt(q[lo:hi], k[lo:hi]), 0.0).astype(bf16)
            total = mm(scores, v[lo:hi])
            if b:
                total = total + mm(mm_nt(q[lo:hi], k[:lo]).astype(bf16), v[:lo])
            intra[lo:hi, cols(h * HDIM)] = total

    loop(0, HEADS, attend)
    pre_send[...] = jnp.zeros_like(pre_send)

    def st_in(j):
        st_copy_of(j, j, partner).wait_recv()
        pre_send[...] += st_all[j].astype(f32)

    loop(0, chip, st_in)
    pre_copy = remote(pre_send, pre_part, one_s.at[4], one_r.at[4], partner)
    pre_copy.start()
    pre_copy.wait_recv()

    for h in range(HEADS):
        lower = core == h // 2

        @pl.when(lower)
        def _():
            st_own[h] = pre_send[h % 2]

        @pl.when(jnp.logical_not(lower))
        def _():
            st_own[h] = pre_part[h % 2]

    @pl.when(core == 0)
    def _():
        pre[...] = st_own[...].astype(bf16)

    @pl.when(core == 1)
    def _():
        pre[...] = (st_own[...] + st_part[...]).astype(bf16)

    def ret_copy(j, slot, n):
        part = cols(n * 256, 256)
        return remote(
            fbuf.at[rows_of(j), part],
            ret.at[rows_of(slot), part],
            s_ret.at[16 * n + j],
            r_ret.at[16 * n + slot],
            member(j),
        )

    def own_ret(n):
        part = cols(n * 256, 256)
        return pltpu.make_async_copy(fbuf.at[rows_of(me), part], ret.at[rows_of(me), part], l_ret.at[n])

    def finish(n):
        for u in range(2):
            at = cols(n * 256 + u * HDIM)
            summed = intra[:, at] + mm(proj[:, at], pre[2 * n + u])
            factor = lax.rsqrt(jnp.mean(summed * summed, axis=-1, keepdims=True) + norm_eps)
            fbuf[:, at] = (summed * factor).astype(bf16)

        def send(m):
            dist = 8 - (m + 1) // 2
            j = wrap(me + jnp.where(m % 2 == 0, dist, MEMS - dist))
            ret_copy(j, me, n).start()

        loop(0, 15, send)
        own_ret(n).start()

    loop(0, 2, finish)

    for g in range(2):

        @pl.when(crosses[g])
        def _():
            kv_copy(g).wait_recv()

    first_pos = seq * TOK

    def window(h):
        for b in range(2):
            lo = b * 128
            q = winq[lo : lo + 128, cols(h * HDIM)]
            k = kv[lo : lo + 640, cols(h * HDIM)]
            v = kv[lo : lo + 640, cols(WIDTH + h * HDIM)]
            scores = mm_nt(q, k) * HDIM ** (-0.5)
            key = lax.broadcasted_iota(jnp.int32, (128, 640), 1)
            distance = lax.broadcasted_iota(jnp.int32, (128, 640), 0) + 2 * TOK - key
            allowed = (distance >= 0) & (distance < WINDOW) & (key + lo + first_pos - 2 * TOK >= 0)
            masked = jnp.where(allowed, scores, -1e30)
            expo = jnp.exp(masked - jnp.max(masked, axis=-1, keepdims=True))
            probs = (expo / jnp.sum(expo, axis=-1, keepdims=True)).astype(bf16)
            wout[lo : lo + 128, cols(h * HDIM)] = mm(probs, v)

    loop(0, HEADS, window)


    def combine(n):
        def ret_in(off):
            j = wrap(me + off)
            ret_copy(j, j, n).wait_recv()

        loop(1, 16, ret_in)
        own_ret(n).wait()
        for u in range(2):
            at = cols(n * 256 + u * HDIM)
            res = ret[:, at]
            g = gcol[...]
            part = g * mm_tn(pick0[...], res) + (1.0 - g) * mm_tn(pick1[...], res)
            out[:, at] = (part + wout[:, at]).astype(bf16)

    loop(0, 2, combine)

    def left(off):
        j = wrap(me + off)
        loop(0, 2, lambda n: ret_copy(j, me, n).wait_send())

        @pl.when(chip < WIN_TILES)
        def _():
            wz_copy(j, me, member(j)).wait_send()
            i = wrap(chip + off)
            remote(wz, wp_block(chip, core), s_wp.at[i], r_wp.at[chip], peer(i)).wait_send()

    loop(1, 16, left)

    def parts_left(k):
        for d in range(2):
            for hop in range(2):
                chain(d, hop, k).wait_send()
            for e in range(6):
                disp_copy(d, e, k).wait_send()

    loop(0, 4, parts_left)
    for d in range(2):
        for hop in range(2):
            slot_chain(d, hop).wait_send()
    for g in range(2):

        @pl.when(crosses[g])
        def _():
            kv_copy(g).wait_send()

    loop(chip + 1, CHIPS, lambda j: st_copy_of(j, chip, peer(j)).wait_send())
    wc_copy.wait_send()
    pre_copy.wait_send()


def shards(tokens, routes, router, mem_weight, win_weight):
    vmem = pl.BlockSpec(memory_space=pltpu.VMEM)
    dma = pltpu.SemaphoreType.DMA
    return pl.pallas_call(
        kernel,
        out_shape=jax.ShapeDtypeStruct((TOK, WIDTH), bf16),
        in_specs=[vmem, vmem, vmem, pl.BlockSpec(memory_space=pl.ANY), vmem],
        out_specs=vmem,
        scratch_shapes=[
            pltpu.VMEM((2, 2, TOK, DEPTH), bf16),
            pltpu.VMEM((2, 2, 2, TOK), jnp.int32),
            pltpu.VMEM((2, 5 * CAP + 32, TOK), bf16),
            pltpu.VMEM((ROWS, TOK), bf16),
            pltpu.VMEM((ROWS, TOK), bf16),
            pltpu.VMEM((2, 5 * CAP + 32, DEPTH), bf16),
            pltpu.VMEM((ROWS, DEPTH), bf16),
            pltpu.VMEM((DEPTH, COLS), bf16),
            pltpu.VMEM((MEMS, 32, 128), bf16),
            pltpu.VMEM((MEMS, 64, COLS), bf16),
            pltpu.VMEM((ROWS, COLS), bf16),
            pltpu.VMEM((ROWS, WIDTH), f32),
            pltpu.VMEM((TOK, WIDTH), bf16),
            pltpu.VMEM((3 * TOK, 2 * WIDTH), bf16),
            pltpu.VMEM((2 * TOK, 2 * WIDTH), bf16),
            pltpu.VMEM((HEADS, HDIM, HDIM), f32),
            pltpu.VMEM((HEADS, HDIM, HDIM), f32),
            pltpu.VMEM((2, HDIM, HDIM), bf16),
            pltpu.VMEM((CHIPS, 2, HDIM, HDIM), bf16),
            pltpu.VMEM((2, HDIM, HDIM), f32),
            pltpu.VMEM((2, HDIM, HDIM), f32),
            pltpu.VMEM((HEADS, HDIM, HDIM), bf16),
            pltpu.VMEM((ROWS, WIDTH), bf16),
            pltpu.VMEM((ROWS, WIDTH), bf16),
            pltpu.VMEM((TOK, WIDTH), f32),
            pltpu.VMEM((TOK, 128), f32),
            pltpu.VMEM((2, TOK), jnp.int32),
        ]
        + [dma((n,)) for n in (16, 16, 4, 4, 48, 64, 4, 32, 32)]
        + [dma((16,))] * 6
        + [dma((5,)), dma((5,)), dma((2,)), dma((2,))],
        compiler_params=pltpu.CompilerParams(
            collective_id=0, has_side_effects=True, vmem_limit_bytes=56 * 1024 * 1024
        ),
    )(tokens, routes.T, router.T, mem_weight, win_weight)


def solution(mesh):
    return jax.shard_map(
        shards,
        mesh=mesh,
        in_specs=(
            P(("ctx", "mem"), None),
            P(("ctx", "mem"), None),
            P(),
            P("mem", None, None),
            P("mem", None),
        ),
        out_specs=P(("ctx", "mem"), None),
        check_vma=False,
    )
```
